512 devices in a mesh: seq: 64 (over z, x), head: 8 (over y, core).
Axes of the slice: x: 4, y: 4, z: 16, core: 2. Of those that a mesh axis runs over, the one named last changes fastest.
Arguments:
- queries: bfloat16 [16384, 8192], P(('seq', 'head')), may hold values from -6 to 6
- key_vectors: bfloat16 [16384, 8192], P(('seq', 'head')), may hold values from -6 to 6
- value_vectors: bfloat16 [16384, 8192], P(('seq', 'head')), may hold values from -6 to 6
- out_grad: bfloat16 [16384, 8192], P(('seq', 'head')), may hold values from -6 to 6
Outputs:
- query_grad: bfloat16 [16384, 8192], P(('seq', 'head'))
- key_grad: bfloat16 [16384, 8192], P(('seq', 'head'))
- value_grad: bfloat16 [16384, 8192], P(('seq', 'head'))
The draws below stay inside these ranges and needn't reach their ends.
All inputs are finite; a program needn't handle non-finite values.
Results may differ from the reference program's by a relative error of at most 0.005.
Values may be sent and summed in bfloat16 or wider, within the bound.
No kernel may reach another device: no remote copies, remote signals or barrier semaphores. Data moves between devices by JAX's collectives and lax.ppermute only.
A program may use at most 192 MiB of HBM per device.

```python
import jax
import jax.numpy as jnp
from jax import lax

HEADS = 64
HEAD_DIM = 128
WIDTH = 8192
TOK_DEV = 256
TOKENS = 16384


def levels(stream_key, dims, cuts, low, high):
    factor_of, own = 1.0, jax.random.fold_in(stream_key, 6)
    for dim, blocks in cuts:
        steps = jnp.exp(jax.random.uniform(jax.random.fold_in(own, dim), (blocks,), jnp.float32, low / len(cuts), high / len(cuts)))
        factor_of = factor_of * jnp.repeat(steps, dims[dim] // blocks).reshape([-1 if axis == dim else 1 for axis in range(len(dims))])
    return factor_of


def gaussian(rng, shape, width, limit, pieces=(), kind=jnp.bfloat16):
    drawn = width * jax.random.normal(rng, shape, jnp.float32)
    if pieces:
        drawn = drawn * levels(rng, shape, pieces, -0.22, 0.18)
    return jnp.clip(drawn, -limit, limit).astype(kind)


def setup_inputs(seed: int = 0) -> dict:
    key_of = jax.random.split(jax.random.key(seed), 5)
    queries = gaussian(key_of[0], (TOKENS, WIDTH), 1.0, 6.0, ((0, 512),))
    key_vectors = gaussian(key_of[1], (TOKENS, WIDTH), 1.0, 6.0, ((0, 512),))
    value_vectors = gaussian(key_of[2], (TOKENS, WIDTH), 1.0, 6.0, ((0, 512),))
    out_grad = gaussian(key_of[3], (TOKENS, WIDTH), 1.0, 6.0, ((0, 512),))
    return {"queries": queries, "key_vectors": key_vectors, "value_vectors": value_vectors, "out_grad": out_grad}


def reference(queries, key_vectors, value_vectors, out_grad):
    f32 = jnp.float32
    hi = lax.Precision.HIGHEST
    nblocks = TOKENS // TOK_DEV
    position = jnp.arange(TOKENS, dtype=f32)
    factor = lax.rsqrt(HEAD_DIM * (position + 1.0))
    scaled = (out_grad.astype(f32) * factor[:, None]).astype(jnp.bfloat16)

    def split(x):
        return x.reshape(nblocks, TOK_DEV, HEADS, HEAD_DIM)
    q_all = split(queries)
    k_all = split(key_vectors)
    v_all = split(value_vectors)
    g_all = split(scaled)

    def block_states(items):
        qb, kb, vb, gb = items
        kv_sum = jnp.einsum('thd,the->hde', kb.astype(f32), vb.astype(f32), precision=hi)
        qg_sum = jnp.einsum('thd,the->hde', qb.astype(f32), gb.astype(f32), precision=hi)
        return (kv_sum, qg_sum)
    kv_all, qg_all = lax.map(block_states, (q_all, k_all, v_all, g_all))
    zero_state = jnp.zeros((1, HEADS, HEAD_DIM, HEAD_DIM), f32)
    prefix = jnp.concatenate([zero_state, jnp.cumsum(kv_all, axis=0)[:-1]], axis=0)
    suffix = jnp.concatenate([jnp.cumsum(qg_all[::-1], axis=0)[:-1][::-1], zero_state], axis=0)
    index = jnp.arange(TOK_DEV, dtype=jnp.int32)
    keep = index[:, None] >= index[None, :]

    def block_grads(items):
        qb, kb, vb, gb, before, after = items
        qf = qb.astype(f32)
        kf = kb.astype(f32)
        vf = vb.astype(f32)
        gf = gb.astype(f32)
        inner = jnp.where(keep[None], jnp.einsum('the,she->hts', gf, vf, precision=hi), 0.0).astype(jnp.bfloat16).astype(f32)
        pairs = jnp.where(keep[None], jnp.einsum('thd,shd->hts', qf, kf, precision=hi), 0.0).astype(jnp.bfloat16).astype(f32)
        dq = jnp.einsum('hts,shd->thd', inner, kf, precision=hi) + jnp.einsum('the,hde->thd', gf, before, precision=hi)
        dk = jnp.einsum('hts,thd->shd', inner, qf, precision=hi) + jnp.einsum('she,hde->shd', vf, after, precision=hi)
        dv = jnp.einsum('hts,the->she', pairs, gf, precision=hi) + jnp.einsum('shd,hde->she', kf, after, precision=hi)
        shape = (TOK_DEV, HEADS * HEAD_DIM)
        return (dq.reshape(shape).astype(jnp.bfloat16), dk.reshape(shape).astype(jnp.bfloat16), dv.reshape(shape).astype(jnp.bfloat16))
    dq_all, dk_all, dv_all = lax.map(block_grads, (q_all, k_all, v_all, g_all, prefix, suffix))
    full = (TOKENS, HEADS * HEAD_DIM)
    return (dq_all.reshape(full), dk_all.reshape(full), dv_all.reshape(full))
```

```python
import functools

import jax
import jax.numpy as jnp
from jax import lax
from jax.experimental import pallas as pl
from jax.experimental.pallas import tpu as pltpu
from jax.sharding import Mesh, PartitionSpec as P

HEAD_DIM = 128
ROWS = 32
CHUNK = 256
AXES = ("zh", "zl", "x", "y", "c")
GROUP = ("zl", "x", "y", "c")
F32 = jnp.float32
BF16 = jnp.bfloat16


def dot(a, b, ca, cb):
    return lax.dot_general(a, b, (((ca,), (cb,)), ((), ())), preferred_element_type=F32)


def params(*names):
    return pltpu.CompilerParams(
        dimension_semantics=("arbitrary",) * len(names), vmem_limit_bytes=48 * 1024 * 1024
    )


def split(x):
    high = x.astype(BF16)
    return high, (x - high.astype(F32)).astype(BF16)


def pack_kernel(q_ref, k_ref, v_ref, g_ref, o_ref):
    for a, ref in enumerate((q_ref, k_ref, v_ref, g_ref)):
        for j in range(o_ref.shape[0]):
            o_ref[j, a] = ref[:, j * HEAD_DIM : (j + 1) * HEAD_DIM]


def pack(q, k, v, g):
    rows, width = q.shape
    heads = width // HEAD_DIM
    step = 16
    return pl.pallas_call(
        pack_kernel,
        grid=(heads // step,),
        in_specs=[pl.BlockSpec((rows, step * HEAD_DIM), lambda i: (0, i))] * 4,
        out_specs=pl.BlockSpec((step, 4, rows, HEAD_DIM), lambda i: (i, 0, 0, 0)),
        out_shape=jax.ShapeDtypeStruct((heads, 4, rows, HEAD_DIM), q.dtype),
        compiler_params=params("i"),
        name="pack",
    )(q, k, v, g)


def unpack_kernel(x_ref, *o_refs):
    for a, ref in enumerate(o_refs):
        for j in range(x_ref.shape[0]):
            ref[:, j * HEAD_DIM : (j + 1) * HEAD_DIM] = x_ref[j, a]


def unpack(x):
    heads, n, rows, _ = x.shape
    step = 16
    return pl.pallas_call(
        unpack_kernel,
        grid=(heads // step,),
        in_specs=[pl.BlockSpec((step, n, rows, HEAD_DIM), lambda i: (i, 0, 0, 0))],
        out_specs=[pl.BlockSpec((rows, step * HEAD_DIM), lambda i: (0, i))] * n,
        out_shape=[jax.ShapeDtypeStruct((rows, heads * HEAD_DIM), x.dtype)] * n,
        compiler_params=params("i"),
        name="unpack",
    )(x)


def part(x_ref, a):
    return x_ref[:, a].reshape(CHUNK, HEAD_DIM)


def scaled_of(x_ref, me_ref, chunks):
    first = me_ref[0] * (chunks * CHUNK) + pl.program_id(0) * CHUNK
    place = lax.broadcasted_iota(jnp.int32, (CHUNK, HEAD_DIM), 0) + first
    factor = lax.rsqrt(HEAD_DIM * (place.astype(F32) + 1.0))
    return (part(x_ref, 3).astype(F32) * factor).astype(BF16)


def sums_kernel(me_ref, x_ref, slots_ref, pre_ref, suf_ref, kv_ref):
    i = pl.program_id(0)
    chunks = pl.num_programs(0)

    @pl.when(i == 0)
    def _():
        kv_ref[...] = jnp.zeros_like(kv_ref)

    g = scaled_of(x_ref, me_ref, chunks)
    pre_ref[i] = kv_ref[...]
    kv_ref[...] += dot(part(x_ref, 1), part(x_ref, 2), 0, 0)
    suf_ref[i] = dot(part(x_ref, 0), g, 0, 0)

    @pl.when(i == chunks - 1)
    def _():
        total = jnp.zeros((HEAD_DIM, HEAD_DIM), F32)
        for c in reversed(range(suf_ref.shape[0])):
            here = suf_ref[c]
            suf_ref[c] = total
            total = total + here
        kv = kv_ref[...].astype(BF16)
        qg = total.astype(BF16)
        for j in range(slots_ref.shape[0]):
            slots_ref[j] = jnp.where(j > me_ref[0], kv, qg)


def sums(me, x, blocks):
    heads = x.shape[0]
    step = CHUNK // ROWS
    chunks = heads // step
    state = (HEAD_DIM, HEAD_DIM)
    whole = lambda i: (0, 0, 0)
    return pl.pallas_call(
        sums_kernel,
        grid=(chunks,),
        in_specs=[
            pl.BlockSpec(memory_space=pltpu.SMEM),
            pl.BlockSpec((step, 4, ROWS, HEAD_DIM), lambda i: (i, 0, 0, 0)),
        ],
        out_specs=[
            pl.BlockSpec((blocks, *state), whole),
            pl.BlockSpec((chunks, *state), whole),
            pl.BlockSpec((chunks, *state), whole),
        ],
        out_shape=[
            jax.ShapeDtypeStruct((blocks, *state), BF16),
            jax.ShapeDtypeStruct((chunks, *state), F32),
            jax.ShapeDtypeStruct((chunks, *state), F32),
        ],
        scratch_shapes=[pltpu.VMEM(state, F32)],
        compiler_params=params("i"),
        name="sums",
    )(me, x)


def near_kernel(me_ref, x_ref, pre_ref, suf_ref, dq_ref, dk_ref, dv_ref):
    q, k, v = part(x_ref, 0), part(x_ref, 1), part(x_ref, 2)
    g = scaled_of(x_ref, me_ref, pl.num_programs(0))
    t = lax.broadcasted_iota(jnp.int32, (CHUNK, CHUNK), 0)
    s = lax.broadcasted_iota(jnp.int32, (CHUNK, CHUNK), 1)
    keep = t >= s
    inner = jnp.where(keep, dot(g, v, 1, 1), 0.0).astype(BF16)
    pairs = jnp.where(keep, dot(q, k, 1, 1), 0.0).astype(BF16)
    pre = split(pre_ref[0])
    suf = split(suf_ref[0])
    dq_ref[...] = dot(inner, k, 1, 0) + (dot(g, pre[0], 1, 1) + dot(g, pre[1], 1, 1))
    dk_ref[...] = dot(inner, q, 0, 0) + (dot(v, suf[0], 1, 1) + dot(v, suf[1], 1, 1))
    dv_ref[...] = dot(pairs, g, 0, 0) + (dot(k, suf[0], 1, 0) + dot(k, suf[1], 1, 0))


def near(me, x, pre, suf):
    heads = x.shape[0]
    step = CHUNK // ROWS
    chunks = heads // step
    state = pl.BlockSpec((1, HEAD_DIM, HEAD_DIM), lambda i: (i, 0, 0))
    rows = pl.BlockSpec((CHUNK, HEAD_DIM), lambda i: (i, 0))
    return pl.pallas_call(
        near_kernel,
        grid=(chunks,),
        in_specs=[
            pl.BlockSpec(memory_space=pltpu.SMEM),
            pl.BlockSpec((step, 4, ROWS, HEAD_DIM), lambda i: (i, 0, 0, 0)),
            state,
            state,
        ],
        out_specs=[rows] * 3,
        out_shape=[jax.ShapeDtypeStruct((chunks * CHUNK, HEAD_DIM), F32)] * 3,
        compiler_params=params("i"),
        cost_estimate=pl.CostEstimate(flops=3_000_000_000, transcendentals=0, bytes_accessed=8 << 20),
        name="near",
    )(me, x, pre, suf)


def far_kernel(me_ref, x_ref, got_ref, dq_ref, dk_ref, dv_ref, o_ref, before_ref, after_ref):
    @pl.when(pl.program_id(0) == 0)
    def _():
        me = me_ref[0]
        before = jnp.zeros((HEAD_DIM, HEAD_DIM), F32)
        after = jnp.zeros((HEAD_DIM, HEAD_DIM), F32)
        for j in range(got_ref.shape[0]):
            here = got_ref[j].astype(F32)
            before = before + jnp.where(j < me, here, 0.0)
            after = after + jnp.where(j > me, here, 0.0)
        for n, value in enumerate(split(before)):
            before_ref[n] = value
        for n, value in enumerate(split(after)):
            after_ref[n] = value

    k, v = part(x_ref, 1), part(x_ref, 2)
    g = scaled_of(x_ref, me_ref, pl.num_programs(0))
    shape = (CHUNK // ROWS, ROWS, HEAD_DIM)
    dq = dq_ref[...] + (dot(g, before_ref[0], 1, 1) + dot(g, before_ref[1], 1, 1))
    dk = dk_ref[...] + (dot(v, after_ref[0], 1, 1) + dot(v, after_ref[1], 1, 1))
    dv = dv_ref[...] + (dot(k, after_ref[0], 1, 0) + dot(k, after_ref[1], 1, 0))
    for a, value in enumerate((dq, dk, dv)):
        o_ref[:, a] = value.astype(BF16).reshape(shape)


def far(me, x, got, dq, dk, dv):
    heads = x.shape[0]
    step = CHUNK // ROWS
    chunks = heads // step
    rows = pl.BlockSpec((CHUNK, HEAD_DIM), lambda i: (i, 0))
    pair = pltpu.VMEM((2, HEAD_DIM, HEAD_DIM), BF16)
    return pl.pallas_call(
        far_kernel,
        grid=(chunks,),
        in_specs=[
            pl.BlockSpec(memory_space=pltpu.SMEM),
            pl.BlockSpec((step, 4, ROWS, HEAD_DIM), lambda i: (i, 0, 0, 0)),
            pl.BlockSpec(got.shape, lambda i: (0, 0, 0)),
            rows,
            rows,
            rows,
        ],
        out_specs=pl.BlockSpec((step, 3, ROWS, HEAD_DIM), lambda i: (i, 0, 0, 0)),
        out_shape=jax.ShapeDtypeStruct((heads, 3, ROWS, HEAD_DIM), BF16),
        scratch_shapes=[pair, pair],
        compiler_params=params("i"),
        name="far",
    )(me, x, got, dq, dk, dv)


def swap(x, axis):
    return lax.all_to_all(x, axis, split_axis=0, concat_axis=0, tiled=True)


def local(queries, key_vectors, value_vectors, out_grad):
    me = lax.axis_index("zh").astype(jnp.int32).reshape(1)
    x = swap(pack(queries, key_vectors, value_vectors, out_grad), GROUP)
    slots, pre, suf = sums(me, x, lax.axis_size("zh"))
    got = swap(slots, "zh")
    dq, dk, dv = near(me, x, pre, suf)
    return tuple(unpack(swap(far(me, x, got, dq, dk, dv), GROUP)))


def solution(mesh):
    fine = Mesh(mesh.devices.reshape(8, 2, 4, 4, 2), AXES)
    spec = P(AXES, None)
    return jax.shard_map(
        local, mesh=fine, in_specs=(spec,) * 4, out_specs=(spec,) * 3, check_vma=False
    )
```

```python
import jax
import jax.numpy as jnp
from jax import lax
from jax.experimental import pallas as pl
from jax.experimental.pallas import tpu as pltpu
from jax.sharding import Mesh, PartitionSpec as P

HEAD_DIM = 128
ROWS = 32
CHUNK = 256
STEP = CHUNK // ROWS
PIECES = 4
AXES = ("zh", "zl", "x", "y", "c")
GROUP = ("zl", "x", "y", "c")
F32 = jnp.float32
BF16 = jnp.bfloat16


def dot(a, b, ca, cb):
    return lax.dot_general(a, b, (((ca,), (cb,)), ((), ())), preferred_element_type=F32)


def params(*names):
    return pltpu.CompilerParams(
        dimension_semantics=("arbitrary",) * len(names), vmem_limit_bytes=16 * 1024 * 1024
    )


def split(x):
    high = x.astype(BF16)
    return high, (x - high.astype(F32)).astype(BF16)


def pack_kernel(first_ref, *refs):
    ins, (o_ref, held, made, in_sem, out_sem) = refs[:4], refs[4:]
    _, rows, width = held.shape
    columns = width // PIECES
    heads = columns // HEAD_DIM

    def fetch(p, a):
        at = (slice(None), pl.ds(p * columns, columns))
        return pltpu.make_async_copy(ins[a].at[at], held.at[(a, *at)], in_sem.at[p, a])

    def send(p):
        at = pl.ds(p * heads, heads)
        return pltpu.make_async_copy(made.at[at], o_ref.at[at], out_sem.at[p])

    for p in range(PIECES):
        for a in range(4):
            fetch(p, a).start()
    place = lax.broadcasted_iota(jnp.int32, (rows, HEAD_DIM), 0) + first_ref[0]
    factor = lax.rsqrt(HEAD_DIM * (place.astype(F32) + 1.0))
    for p in range(PIECES):
        for a in range(4):
            fetch(p, a).wait()
        for h in range(p * heads, (p + 1) * heads):
            at = slice(h * HEAD_DIM, (h + 1) * HEAD_DIM)
            made[h, 0] = held[0, :, at]
            made[h, 1] = held[1, :, at]
            made[h, 2] = (held[2, :, at].astype(F32) * factor).astype(BF16)
            made[h, 3] = held[3, :, at]
        send(p).start()
    for p in range(PIECES):
        send(p).wait()


def pack(first, *arrays):
    rows, width = arrays[0].shape
    shape = (width // HEAD_DIM, 4, rows, HEAD_DIM)
    arrays = [pltpu.with_memory_space_constraint(y, pltpu.HBM) for y in arrays]
    return pl.pallas_call(
        pack_kernel,
        in_specs=[pl.BlockSpec(memory_space=pltpu.SMEM)]
        + [pl.BlockSpec(memory_space=pltpu.HBM)] * 4,
        out_specs=pl.BlockSpec(memory_space=pltpu.HBM),
        out_shape=pltpu.HBM(shape, BF16),
        scratch_shapes=[
            pltpu.VMEM((4, rows, width), BF16),
            pltpu.VMEM(shape, BF16),
            pltpu.SemaphoreType.DMA((PIECES, 4)),
            pltpu.SemaphoreType.DMA((PIECES,)),
        ],
        compiler_params=params(),
        name="pack",
    )(first, *arrays)


def unpack_kernel(x_ref, *refs):
    outs, (made, sem) = refs[:3], refs[3:]
    width = made.shape[2]
    columns = width // PIECES
    heads = columns // HEAD_DIM

    def send(p, a):
        at = (slice(None), pl.ds(p * columns, columns))
        return pltpu.make_async_copy(made.at[(a, *at)], outs[a].at[at], sem.at[p, a])

    for p in range(PIECES):
        for a in range(3):
            for h in range(p * heads, (p + 1) * heads):
                made[a, :, h * HEAD_DIM : (h + 1) * HEAD_DIM] = x_ref[h, a]
            send(p, a).start()
    for p in range(PIECES):
        for a in range(3):
            send(p, a).wait()


def unpack(x):
    heads, n, rows, _ = x.shape
    width = heads * HEAD_DIM
    return pl.pallas_call(
        unpack_kernel,
        in_specs=[pl.BlockSpec(memory_space=pltpu.VMEM)],
        out_specs=[pl.BlockSpec(memory_space=pltpu.HBM)] * n,
        out_shape=[pltpu.HBM((rows, width), x.dtype)] * n,
        scratch_shapes=[
            pltpu.VMEM((n, rows, width), x.dtype),
            pltpu.SemaphoreType.DMA((PIECES, n)),
        ],
        compiler_params=params(),
        name="unpack",
    )(x)


def rows_of(x_ref, a, c=None):
    x = x_ref[:, a] if c is None else x_ref[c * STEP : (c + 1) * STEP, a]
    return x.reshape(-1, HEAD_DIM)


def sums_kernel(me_ref, x_ref, slots_ref):
    kv = dot(rows_of(x_ref, 0), rows_of(x_ref, 1), 0, 0).astype(BF16)
    qg = dot(rows_of(x_ref, 3), rows_of(x_ref, 2), 0, 0).astype(BF16)
    for j in range(slots_ref.shape[0]):
        slots_ref[j] = jnp.where(j > me_ref[0], kv, qg)


def sums(me, x, blocks):
    return pl.pallas_call(
        sums_kernel,
        in_specs=[
            pl.BlockSpec(memory_space=pltpu.SMEM),
            pl.BlockSpec(memory_space=pltpu.VMEM),
        ],
        out_specs=pl.BlockSpec(memory_space=pltpu.VMEM),
        out_shape=jax.ShapeDtypeStruct((blocks, HEAD_DIM, HEAD_DIM), BF16),
        compiler_params=params(),
        name="sums",
    )(me, x)


def near_kernel(x_ref, dq_ref, dk_ref, dv_ref, kv_ref, suf_ref):
    i = pl.program_id(0)
    chunks = suf_ref.shape[0]

    @pl.when(i == 0)
    def _():
        kv_ref[...] = jnp.zeros_like(kv_ref)
        after = jnp.zeros((HEAD_DIM, HEAD_DIM), F32)
        for c in reversed(range(chunks)):
            suf_ref[c] = after
            if c:
                after = after + dot(rows_of(x_ref, 3, c), rows_of(x_ref, 2, c), 0, 0)

    at = pl.ds(i * STEP, STEP)
    k, v, g, q = (x_ref[at, a].reshape(CHUNK, HEAD_DIM) for a in range(4))
    t = lax.broadcasted_iota(jnp.int32, (CHUNK, CHUNK), 0)
    s = lax.broadcasted_iota(jnp.int32, (CHUNK, CHUNK), 1)
    keep = t >= s
    inner = jnp.where(keep, dot(g, v, 1, 1), 0.0).astype(BF16)
    pairs = jnp.where(keep, dot(q, k, 1, 1), 0.0).astype(BF16)
    pre = split(kv_ref[...])
    suf = split(suf_ref[i])
    dq_ref[...] = dot(inner, k, 1, 0) + (dot(g, pre[0], 1, 1) + dot(g, pre[1], 1, 1))
    dk_ref[...] = dot(inner, q, 0, 0) + (dot(v, suf[0], 1, 1) + dot(v, suf[1], 1, 1))
    dv_ref[...] = dot(pairs, g, 0, 0) + (dot(k, suf[0], 1, 0) + dot(k, suf[1], 1, 0))
    kv_ref[...] += dot(k, v, 0, 0)


def near(x):
    chunks = x.shape[0] // STEP
    rows = pl.BlockSpec((CHUNK, HEAD_DIM), lambda i: (i, 0))
    return pl.pallas_call(
        near_kernel,
        grid=(chunks,),
        in_specs=[pl.BlockSpec(memory_space=pltpu.VMEM)],
        out_specs=[rows] * 3,
        out_shape=[pltpu.HBM((chunks * CHUNK, HEAD_DIM), F32)] * 3,
        scratch_shapes=[
            pltpu.VMEM((HEAD_DIM, HEAD_DIM), F32),
            pltpu.VMEM((chunks, HEAD_DIM, HEAD_DIM), F32),
        ],
        compiler_params=params("i"),
        cost_estimate=pl.CostEstimate(flops=3_000_000_000, transcendentals=0, bytes_accessed=8 << 20),
        name="near",
    )(x)


def far_kernel(me_ref, x_ref, got_ref, *refs):
    ins, (o_ref, held, dq_state, dk_state, dv_state, sem) = refs[:3], refs[3:]
    heads = o_ref.shape[0] // PIECES
    rows = heads * ROWS

    def fetch(p, a):
        at = pl.ds(p * rows, rows)
        return pltpu.make_async_copy(ins[a].at[at], held.at[a, at], sem.at[p, a])

    for p in range(PIECES):
        for a in range(3):
            fetch(p, a).start()
    me = me_ref[0]
    before = jnp.zeros((HEAD_DIM, HEAD_DIM), F32)
    after = jnp.zeros((HEAD_DIM, HEAD_DIM), F32)
    for j in range(got_ref.shape[0]):
        here = got_ref[j].astype(F32)
        before = before + jnp.where(j < me, here, 0.0)
        after = after + jnp.where(j > me, here, 0.0)
    for n, (b, s) in enumerate(zip(split(before), split(after))):
        at = slice(n * HEAD_DIM, (n + 1) * HEAD_DIM)
        dq_state[:, at] = b
        dk_state[:, at] = s
        dv_state[at, :] = s
    for p in range(PIECES):
        for a in range(3):
            fetch(p, a).wait()
        hs = slice(p * heads, (p + 1) * heads)
        rs = slice(p * rows, (p + 1) * rows)
        k, v, g = (x_ref[hs, a].reshape(rows, HEAD_DIM) for a in range(3))
        k, v, g = (jnp.concatenate([y, y], axis=1) for y in (k, v, g))
        dq = held[0, rs] + dot(g, dq_state[...], 1, 1)
        dk = held[1, rs] + dot(v, dk_state[...], 1, 1)
        dv = held[2, rs] + dot(k, dv_state[...], 1, 0)
        for a, value in enumerate((dq, dk, dv)):
            o_ref[hs, a] = value.astype(BF16).reshape(heads, ROWS, HEAD_DIM)


def far(me, x, got, *parts):
    heads = x.shape[0]
    vmem = pl.BlockSpec(memory_space=pltpu.VMEM)
    parts = [pltpu.with_memory_space_constraint(y, pltpu.HBM) for y in parts]
    wide = pltpu.VMEM((HEAD_DIM, 2 * HEAD_DIM), BF16)
    return pl.pallas_call(
        far_kernel,
        in_specs=[pl.BlockSpec(memory_space=pltpu.SMEM), vmem, vmem]
        + [pl.BlockSpec(memory_space=pltpu.HBM)] * 3,
        out_specs=vmem,
        out_shape=jax.ShapeDtypeStruct((heads, 3, ROWS, HEAD_DIM), BF16),
        scratch_shapes=[
            pltpu.VMEM((3, heads * ROWS, HEAD_DIM), F32),
            wide,
            wide,
            pltpu.VMEM((2 * HEAD_DIM, HEAD_DIM), BF16),
            pltpu.SemaphoreType.DMA((PIECES, 3)),
        ],
        compiler_params=params(),
        name="far",
    )(me, x, got, *parts)


def swap(x, axis):
    return lax.all_to_all(x, axis, split_axis=0, concat_axis=0, tiled=True)


def local(queries, key_vectors, value_vectors, out_grad):
    me = lax.axis_index("zh").astype(jnp.int32).reshape(1)
    first = (lax.axis_index(AXES) * ROWS).astype(jnp.int32).reshape(1)
    x = swap(pack(first, key_vectors, value_vectors, out_grad, queries), GROUP)
    got = swap(sums(me, x, lax.axis_size("zh")), "zh")
    dq, dk, dv = near(x)
    return tuple(unpack(swap(far(me, x, got, dq, dk, dv), GROUP)))


def solution(mesh):
    fine = Mesh(mesh.devices.reshape(8, 2, 4, 4, 2), AXES)
    spec = P(AXES, None)
    return jax.shard_map(
        local, mesh=fine, in_specs=(spec,) * 4, out_specs=(spec,) * 3, check_vma=False
    )
```

```python
import jax
import jax.numpy as jnp
from jax import lax
from jax.experimental import pallas as pl
from jax.experimental.pallas import tpu as pltpu
from jax.sharding import Mesh, PartitionSpec as P

HEAD_DIM = 128
ROWS = 32
CHUNK = 256
STEP = CHUNK // ROWS
PIECES = 4
BLOCKS = "block"
GROUP = "group"
AXES = (BLOCKS, GROUP)
F32 = jnp.float32
BF16 = jnp.bfloat16


def dot(a, b, ca, cb):
    return lax.dot_general(a, b, (((ca,), (cb,)), ((), ())), preferred_element_type=F32)


def params(*names):
    return pltpu.CompilerParams(
        dimension_semantics=("arbitrary",) * len(names), vmem_limit_bytes=16 * 1024 * 1024
    )


def split(x):
    high = x.astype(BF16)
    return high, (x - high.astype(F32)).astype(BF16)


def pack_kernel(first_ref, *refs):
    ins, (o_ref, held, made, in_sem, out_sem) = refs[:4], refs[4:]
    _, rows, width = held.shape
    columns = width // PIECES
    heads = columns // HEAD_DIM

    def fetch(p, a):
        at = (slice(None), pl.ds(p * columns, columns))
        return pltpu.make_async_copy(ins[a].at[at], held.at[(a, *at)], in_sem.at[p, a])

    def send(p):
        at = pl.ds(p * heads, heads)
        return pltpu.make_async_copy(made.at[at], o_ref.at[at], out_sem.at[p])

    for p in range(PIECES):
        for a in range(4):
            fetch(p, a).start()
    place = lax.broadcasted_iota(jnp.int32, (rows, HEAD_DIM), 0) + first_ref[0]
    factor = lax.rsqrt(HEAD_DIM * (place.astype(F32) + 1.0))
    for p in range(PIECES):
        for a in range(4):
            fetch(p, a).wait()
        for h in range(p * heads, (p + 1) * heads):
            at = slice(h * HEAD_DIM, (h + 1) * HEAD_DIM)
            made[h, 0] = held[0, :, at]
            made[h, 1] = held[1, :, at]
            made[h, 2] = (held[2, :, at].astype(F32) * factor).astype(BF16)
            made[h, 3] = held[3, :, at]
        send(p).start()
    for p in range(PIECES):
        send(p).wait()


def pack(first, *arrays):
    rows, width = arrays[0].shape
    shape = (width // HEAD_DIM, 4, rows, HEAD_DIM)
    arrays = [pltpu.with_memory_space_constraint(y, pltpu.HBM) for y in arrays]
    return pl.pallas_call(
        pack_kernel,
        in_specs=[pl.BlockSpec(memory_space=pltpu.SMEM)]
        + [pl.BlockSpec(memory_space=pltpu.HBM)] * 4,
        out_specs=pl.BlockSpec(memory_space=pltpu.HBM),
        out_shape=pltpu.HBM(shape, BF16),
        scratch_shapes=[
            pltpu.VMEM((4, rows, width), BF16),
            pltpu.VMEM(shape, BF16),
            pltpu.SemaphoreType.DMA((PIECES, 4)),
            pltpu.SemaphoreType.DMA((PIECES,)),
        ],
        compiler_params=params(),
        name="pack",
    )(first, *arrays)


def unpack_kernel(x_ref, *refs):
    outs, (made, sem) = refs[:3], refs[3:]
    width = made.shape[2]
    columns = width // PIECES
    heads = columns // HEAD_DIM

    def send(p, a):
        at = (slice(None), pl.ds(p * columns, columns))
        return pltpu.make_async_copy(made.at[(a, *at)], outs[a].at[at], sem.at[p, a])

    for p in range(PIECES):
        for a in range(3):
            for h in range(p * heads, (p + 1) * heads):
                made[a, :, h * HEAD_DIM : (h + 1) * HEAD_DIM] = x_ref[h, a]
            send(p, a).start()
    for p in range(PIECES):
        for a in range(3):
            send(p, a).wait()


def unpack(x):
    heads, n, rows, _ = x.shape
    width = heads * HEAD_DIM
    return pl.pallas_call(
        unpack_kernel,
        in_specs=[pl.BlockSpec(memory_space=pltpu.VMEM)],
        out_specs=[pl.BlockSpec(memory_space=pltpu.HBM)] * n,
        out_shape=[pltpu.HBM((rows, width), x.dtype)] * n,
        scratch_shapes=[
            pltpu.VMEM((n, rows, width), x.dtype),
            pltpu.SemaphoreType.DMA((PIECES, n)),
        ],
        compiler_params=params(),
        name="unpack",
    )(x)


def rows_of(x_ref, a, c=None):
    x = x_ref[:, a] if c is None else x_ref[c * STEP : (c + 1) * STEP, a]
    return x.reshape(-1, HEAD_DIM)


def sums_kernel(me_ref, x_ref, slots_ref):
    kv = dot(rows_of(x_ref, 0), rows_of(x_ref, 1), 0, 0).astype(BF16)
    qg = dot(rows_of(x_ref, 3), rows_of(x_ref, 2), 0, 0).astype(BF16)
    for j in range(slots_ref.shape[0]):
        slots_ref[j] = jnp.where(j > me_ref[0], kv, qg)


def sums(me, x, blocks):
    return pl.pallas_call(
        sums_kernel,
        in_specs=[
            pl.BlockSpec(memory_space=pltpu.SMEM),
            pl.BlockSpec(memory_space=pltpu.VMEM),
        ],
        out_specs=pl.BlockSpec(memory_space=pltpu.VMEM),
        out_shape=jax.ShapeDtypeStruct((blocks, HEAD_DIM, HEAD_DIM), BF16),
        compiler_params=params(),
        name="sums",
    )(me, x)


def near_kernel(x_ref, dq_ref, dk_ref, dv_ref, kv_ref, suf_ref):
    i = pl.program_id(0)
    chunks = suf_ref.shape[0]

    @pl.when(i == 0)
    def _():
        kv_ref[...] = jnp.zeros_like(kv_ref)
        after = jnp.zeros((HEAD_DIM, HEAD_DIM), F32)
        for c in reversed(range(chunks)):
            suf_ref[c] = after
            if c:
                after = after + dot(rows_of(x_ref, 3, c), rows_of(x_ref, 2, c), 0, 0)

    at = pl.ds(i * STEP, STEP)
    k, v, g, q = (x_ref[at, a].reshape(CHUNK, HEAD_DIM) for a in range(4))
    t = lax.broadcasted_iota(jnp.int32, (CHUNK, CHUNK), 0)
    s = lax.broadcasted_iota(jnp.int32, (CHUNK, CHUNK), 1)
    keep = t >= s
    inner = jnp.where(keep, dot(g, v, 1, 1), 0.0).astype(BF16)
    pairs = jnp.where(keep, dot(q, k, 1, 1), 0.0).astype(BF16)
    pre = split(kv_ref[...])
    suf = split(suf_ref[i])
    dq_ref[...] = dot(inner, k, 1, 0) + (dot(g, pre[0], 1, 1) + dot(g, pre[1], 1, 1))
    dk_ref[...] = dot(inner, q, 0, 0) + (dot(v, suf[0], 1, 1) + dot(v, suf[1], 1, 1))
    dv_ref[...] = dot(pairs, g, 0, 0) + (dot(k, suf[0], 1, 0) + dot(k, suf[1], 1, 0))
    kv_ref[...] += dot(k, v, 0, 0)


def near(x):
    chunks = x.shape[0] // STEP
    rows = pl.BlockSpec((CHUNK, HEAD_DIM), lambda i: (i, 0))
    return pl.pallas_call(
        near_kernel,
        grid=(chunks,),
        in_specs=[pl.BlockSpec(memory_space=pltpu.VMEM)],
        out_specs=[rows] * 3,
        out_shape=[jax.ShapeDtypeStruct((chunks * CHUNK, HEAD_DIM), F32)]
        + [pltpu.HBM((chunks * CHUNK, HEAD_DIM), F32)] * 2,
        scratch_shapes=[
            pltpu.VMEM((HEAD_DIM, HEAD_DIM), F32),
            pltpu.VMEM((chunks, HEAD_DIM, HEAD_DIM), F32),
        ],
        compiler_params=params("i"),
        cost_estimate=pl.CostEstimate(flops=3_000_000_000, transcendentals=0, bytes_accessed=8 << 20),
        name="near",
    )(x)


def far_kernel(me_ref, x_ref, got_ref, dq_ref, *refs):
    ins, (o_ref, held, dq_state, dk_state, dv_state, sem) = refs[:2], refs[2:]

    def fetch(a):
        return pltpu.make_async_copy(ins[a], held.at[a], sem.at[a])

    for a in range(2):
        fetch(a).start()
    me = me_ref[0]
    before = jnp.zeros((HEAD_DIM, HEAD_DIM), F32)
    after = jnp.zeros((HEAD_DIM, HEAD_DIM), F32)
    for j in range(got_ref.shape[0]):
        here = got_ref[j].astype(F32)
        before = before + jnp.where(j < me, here, 0.0)
        after = after + jnp.where(j > me, here, 0.0)
    for n, (b, s) in enumerate(zip(split(before), split(after))):
        at = slice(n * HEAD_DIM, (n + 1) * HEAD_DIM)
        dq_state[:, at] = b
        dk_state[:, at] = s
        dv_state[at, :] = s

    def add(out, source, near, state, axis):
        y = rows_of(x_ref, source)
        y = jnp.concatenate([y, y], axis=1)
        value = near[...] + dot(y, state[...], 1, axis)
        o_ref[:, out] = value.astype(BF16).reshape(-1, ROWS, HEAD_DIM)

    add(0, 2, dq_ref, dq_state, 1)
    for a in range(2):
        fetch(a).wait()
    add(1, 1, held.at[0], dk_state, 1)
    add(2, 0, held.at[1], dv_state, 0)


def far(me, x, got, dq, *parts):
    heads = x.shape[0]
    vmem = pl.BlockSpec(memory_space=pltpu.VMEM)
    parts = [pltpu.with_memory_space_constraint(y, pltpu.HBM) for y in parts]
    wide = pltpu.VMEM((HEAD_DIM, 2 * HEAD_DIM), BF16)
    return pl.pallas_call(
        far_kernel,
        in_specs=[pl.BlockSpec(memory_space=pltpu.SMEM), vmem, vmem, vmem]
        + [pl.BlockSpec(memory_space=pltpu.HBM)] * 2,
        out_specs=vmem,
        out_shape=jax.ShapeDtypeStruct((heads, 3, ROWS, HEAD_DIM), BF16),
        scratch_shapes=[
            pltpu.VMEM((2, heads * ROWS, HEAD_DIM), F32),
            wide,
            wide,
            pltpu.VMEM((2 * HEAD_DIM, HEAD_DIM), BF16),
            pltpu.SemaphoreType.DMA((2,)),
        ],
        compiler_params=params(),
        name="far",
    )(me, x, got, dq, *parts)


def swap(x, axis):
    return lax.all_to_all(x, axis, split_axis=0, concat_axis=0, tiled=True)


def local(queries, key_vectors, value_vectors, out_grad):
    me = lax.axis_index(BLOCKS).astype(jnp.int32).reshape(1)
    first = (lax.axis_index(AXES) * ROWS).astype(jnp.int32).reshape(1)
    x = swap(pack(first, key_vectors, value_vectors, out_grad, queries), GROUP)
    got = swap(sums(me, x, lax.axis_size(BLOCKS)), BLOCKS)
    return tuple(unpack(swap(far(me, x, got, *near(x)), GROUP)))


def solution(mesh):
    fine = Mesh(mesh.devices.reshape(8, 64), AXES)
    spec = P(AXES, None)
    return jax.shard_map(
        local, mesh=fine, in_specs=(spec,) * 4, out_specs=(spec,) * 3, check_vma=False
    )
```

```python
import jax
import jax.numpy as jnp
from jax import lax
from jax.experimental import pallas as pl
from jax.experimental.pallas import tpu as pltpu
from jax.sharding import Mesh, PartitionSpec as P

HEAD_DIM = 128
ROWS = 32
CHUNK = 256
STEP = CHUNK // ROWS
PARTS = 2
PIECES = 4
BLOCKS = "block"
GROUP = "group"
AXES = (BLOCKS, GROUP)
F32 = jnp.float32
BF16 = jnp.bfloat16


def dot(a, b, ca, cb):
    return lax.dot_general(a, b, (((ca,), (cb,)), ((), ())), preferred_element_type=F32)


def params(*names):
    return pltpu.CompilerParams(
        dimension_semantics=("arbitrary",) * len(names), vmem_limit_bytes=16 * 1024 * 1024
    )


def split(x):
    high = x.astype(BF16)
    return high, (x - high.astype(F32)).astype(BF16)


def pack_kernel(first_ref, *refs):
    ins, (o_ref, held, made, in_sem, out_sem) = refs[:4], refs[4:]
    _, rows, width = held.shape
    columns = width // PIECES
    heads = columns // HEAD_DIM

    def fetch(p, a):
        at = (slice(None), pl.ds(p * columns, columns))
        return pltpu.make_async_copy(ins[a].at[at], held.at[(a, *at)], in_sem.at[p, a])

    def send(p):
        at = pl.ds(p * heads, heads)
        return pltpu.make_async_copy(made.at[at], o_ref.at[at], out_sem.at[p])

    for p in range(PIECES):
        for a in range(4):
            fetch(p, a).start()
    place = lax.broadcasted_iota(jnp.int32, (rows, HEAD_DIM), 0) + first_ref[0]
    factor = lax.rsqrt(HEAD_DIM * (place.astype(F32) + 1.0))
    for p in range(PIECES):
        for a in range(4):
            fetch(p, a).wait()
        for h in range(p * heads, (p + 1) * heads):
            at = slice(h * HEAD_DIM, (h + 1) * HEAD_DIM)
            made[h, 0] = held[0, :, at]
            made[h, 1] = held[1, :, at]
            made[h, 2] = (held[2, :, at].astype(F32) * factor).astype(BF16)
            made[h, 3] = held[3, :, at]
        send(p).start()
    for p in range(PIECES):
        send(p).wait()


def pack(first, *arrays):
    rows, width = arrays[0].shape
    shape = (width // HEAD_DIM, 4, rows, HEAD_DIM)
    arrays = [pltpu.with_memory_space_constraint(y, pltpu.HBM) for y in arrays]
    return pl.pallas_call(
        pack_kernel,
        in_specs=[pl.BlockSpec(memory_space=pltpu.SMEM)]
        + [pl.BlockSpec(memory_space=pltpu.HBM)] * 4,
        out_specs=pl.BlockSpec(memory_space=pltpu.HBM),
        out_shape=pltpu.HBM(shape, BF16),
        scratch_shapes=[
            pltpu.VMEM((4, rows, width), BF16),
            pltpu.VMEM(shape, BF16),
            pltpu.SemaphoreType.DMA((PIECES, 4)),
            pltpu.SemaphoreType.DMA((PIECES,)),
        ],
        compiler_params=params(),
        name="pack",
    )(first, *arrays)


def unpack_kernel(x_ref, *refs):
    outs, (made, sem) = refs[:3], refs[3:]
    width = made.shape[2]
    columns = width // PIECES
    heads = columns // HEAD_DIM

    def send(p, a):
        at = (slice(None), pl.ds(p * columns, columns))
        return pltpu.make_async_copy(made.at[(a, *at)], outs[a].at[at], sem.at[p, a])

    for p in range(PIECES):
        for a in range(3):
            for h in range(p * heads, (p + 1) * heads):
                made[a, :, h * HEAD_DIM : (h + 1) * HEAD_DIM] = x_ref[h, a]
            send(p, a).start()
    for p in range(PIECES):
        for a in range(3):
            send(p, a).wait()


def unpack(x):
    heads, n, rows, _ = x.shape
    width = heads * HEAD_DIM
    return pl.pallas_call(
        unpack_kernel,
        in_specs=[pl.BlockSpec(memory_space=pltpu.VMEM)],
        out_specs=[pl.BlockSpec(memory_space=pltpu.HBM)] * n,
        out_shape=[pltpu.HBM((rows, width), x.dtype)] * n,
        scratch_shapes=[
            pltpu.VMEM((n, rows, width), x.dtype),
            pltpu.SemaphoreType.DMA((PIECES, n)),
        ],
        compiler_params=params(),
        name="unpack",
    )(x)


def rows_of(x_ref, a, c=None):
    x = x_ref[:, a] if c is None else x_ref[c * STEP : (c + 1) * STEP, a]
    return x.reshape(-1, HEAD_DIM)


def sums_kernel(me_ref, x_ref, slots_ref):
    kv = dot(rows_of(x_ref, 0), rows_of(x_ref, 1), 0, 0).astype(BF16)
    qg = dot(rows_of(x_ref, 3), rows_of(x_ref, 2), 0, 0).astype(BF16)
    for j in range(slots_ref.shape[0]):
        slots_ref[j] = jnp.where(j > me_ref[0], kv, qg)


def sums(me, x, blocks):
    return pl.pallas_call(
        sums_kernel,
        in_specs=[
            pl.BlockSpec(memory_space=pltpu.SMEM),
            pl.BlockSpec(memory_space=pltpu.VMEM),
        ],
        out_specs=pl.BlockSpec(memory_space=pltpu.VMEM),
        out_shape=jax.ShapeDtypeStruct((blocks, HEAD_DIM, HEAD_DIM), BF16),
        compiler_params=params(),
        name="sums",
    )(me, x)


def near_kernel(x_ref, dq_ref, dk_ref, dv_ref, kv_ref, suf_ref):
    i = pl.program_id(0)
    chunks = suf_ref.shape[0]

    @pl.when(i == 0)
    def _():
        kv_ref[...] = jnp.zeros_like(kv_ref)
        after = jnp.zeros((HEAD_DIM, HEAD_DIM), F32)
        for c in reversed(range(chunks)):
            suf_ref[c] = after
            if c:
                after = after + dot(rows_of(x_ref, 3, c), rows_of(x_ref, 2, c), 0, 0)

    at = pl.ds(i * STEP, STEP)
    k, v, g, q = (x_ref[at, a].reshape(CHUNK, HEAD_DIM) for a in range(4))
    t = lax.broadcasted_iota(jnp.int32, (CHUNK, CHUNK), 0)
    s = lax.broadcasted_iota(jnp.int32, (CHUNK, CHUNK), 1)
    keep = t >= s
    inner = jnp.where(keep, dot(g, v, 1, 1), 0.0).astype(BF16)
    pairs = jnp.where(keep, dot(q, k, 1, 1), 0.0).astype(BF16)
    pre = split(kv_ref[...])
    suf = split(suf_ref[i])
    dq_ref[...] = dot(inner, k, 1, 0) + (dot(g, pre[0], 1, 1) + dot(g, pre[1], 1, 1))
    dk_ref[...] = dot(inner, q, 0, 0) + (dot(v, suf[0], 1, 1) + dot(v, suf[1], 1, 1))
    dv_ref[...] = dot(pairs, g, 0, 0) + (dot(k, suf[0], 1, 0) + dot(k, suf[1], 1, 0))
    kv_ref[...] += dot(k, v, 0, 0)


def near(x):
    chunks = x.shape[0] // STEP
    rows = pl.BlockSpec((CHUNK, HEAD_DIM), lambda i: (i, 0))
    return pl.pallas_call(
        near_kernel,
        grid=(chunks,),
        in_specs=[pl.BlockSpec(memory_space=pltpu.VMEM)],
        out_specs=[rows] * 3,
        out_shape=[jax.ShapeDtypeStruct((chunks * CHUNK, HEAD_DIM), F32)]
        + [pltpu.HBM((chunks * CHUNK, HEAD_DIM), F32)] * 2,
        scratch_shapes=[
            pltpu.VMEM((HEAD_DIM, HEAD_DIM), F32),
            pltpu.VMEM((chunks, HEAD_DIM, HEAD_DIM), F32),
        ],
        compiler_params=params("i"),
        cost_estimate=pl.CostEstimate(flops=3_000_000_000, transcendentals=0, bytes_accessed=8 << 20),
        name="near",
    )(x)


def far_kernel(me_ref, x_ref, got_ref, dq_ref, *refs):
    ins, (o_ref, held, dq_state, dk_state, dv_state, sem) = refs[:2], refs[2:]

    def fetch(a):
        return pltpu.make_async_copy(ins[a], held.at[a], sem.at[a])

    for a in range(2):
        fetch(a).start()
    me = me_ref[0]
    before = jnp.zeros((HEAD_DIM, HEAD_DIM), F32)
    after = jnp.zeros((HEAD_DIM, HEAD_DIM), F32)
    for j in range(got_ref.shape[0]):
        here = got_ref[j].astype(F32)
        before = before + jnp.where(j < me, here, 0.0)
        after = after + jnp.where(j > me, here, 0.0)
    for n, (b, s) in enumerate(zip(split(before), split(after))):
        at = slice(n * HEAD_DIM, (n + 1) * HEAD_DIM)
        dq_state[:, at] = b
        dk_state[:, at] = s
        dv_state[:, at] = s.T

    rows = held.shape[1] // PARTS

    def add(p, out, source, near, state):
        y = x_ref[p * (rows // ROWS) : (p + 1) * (rows // ROWS), source].reshape(rows, HEAD_DIM)
        y = jnp.concatenate([y, y], axis=1)
        value = near[p * rows : (p + 1) * rows] + dot(y, state[...], 1, 1)
        o_ref[p * (rows // ROWS) : (p + 1) * (rows // ROWS), out] = value.astype(BF16).reshape(-1, ROWS, HEAD_DIM)

    for p in range(PARTS):
        add(p, 0, 2, dq_ref, dq_state)
    for a in range(2):
        fetch(a).wait()
    for p in range(PARTS):
        add(p, 1, 1, held.at[0], dk_state)
    for p in range(PARTS):
        add(p, 2, 0, held.at[1], dv_state)


def far(me, x, got, dq, *parts):
    heads = x.shape[0]
    vmem = pl.BlockSpec(memory_space=pltpu.VMEM)
    parts = [pltpu.with_memory_space_constraint(y, pltpu.HBM) for y in parts]
    wide = pltpu.VMEM((HEAD_DIM, 2 * HEAD_DIM), BF16)
    return pl.pallas_call(
        far_kernel,
        in_specs=[pl.BlockSpec(memory_space=pltpu.SMEM), vmem, vmem, vmem]
        + [pl.BlockSpec(memory_space=pltpu.HBM)] * 2,
        out_specs=vmem,
        out_shape=jax.ShapeDtypeStruct((heads, 3, ROWS, HEAD_DIM), BF16),
        scratch_shapes=[
            pltpu.VMEM((2, heads * ROWS, HEAD_DIM), F32),
            wide,
            wide,
            wide,
            pltpu.SemaphoreType.DMA((2,)),
        ],
        compiler_params=params(),
        name="far",
    )(me, x, got, dq, *parts)


def swap(x, axis):
    return lax.all_to_all(x, axis, split_axis=0, concat_axis=0, tiled=True)


def local(queries, key_vectors, value_vectors, out_grad):
    me = lax.axis_index(BLOCKS).astype(jnp.int32).reshape(1)
    first = (lax.axis_index(AXES) * ROWS).astype(jnp.int32).reshape(1)
    x = swap(pack(first, key_vectors, value_vectors, out_grad, queries), GROUP)
    got = swap(sums(me, x, lax.axis_size(BLOCKS)), BLOCKS)
    return tuple(unpack(swap(far(me, x, got, *near(x)), GROUP)))


def solution(mesh):
    fine = Mesh(mesh.devices.reshape(8, 64), AXES)
    spec = P(AXES, None)
    return jax.shard_map(
        local, mesh=fine, in_specs=(spec,) * 4, out_specs=(spec,) * 3, check_vma=False
    )
```

```python
import jax
import jax.numpy as jnp
from jax import lax
from jax.experimental import pallas as pl
from jax.experimental.pallas import tpu as pltpu
from jax.sharding import Mesh, PartitionSpec as P

HEAD_DIM = 128
ROWS = 32
CHUNK = 256
STEP = CHUNK // ROWS
PIECES = 2
BLOCKS = "block"
GROUP = "group"
AXES = (BLOCKS, GROUP)
F32 = jnp.float32
BF16 = jnp.bfloat16


def dot(a, b, ca, cb):
    return lax.dot_general(a, b, (((ca,), (cb,)), ((), ())), preferred_element_type=F32)


def params(*names):
    return pltpu.CompilerParams(
        dimension_semantics=("arbitrary",) * len(names), vmem_limit_bytes=16 * 1024 * 1024
    )


def split(x):
    high = x.astype(BF16)
    return high, (x - high.astype(F32)).astype(BF16)


def pack_kernel(first_ref, *refs):
    ins, (o_ref, held, made, in_sem, out_sem) = refs[:4], refs[4:]
    _, rows, width = held.shape
    columns = width // PIECES
    heads = columns // HEAD_DIM

    def fetch(p, a):
        at = (slice(None), pl.ds(p * columns, columns))
        return pltpu.make_async_copy(ins[a].at[at], held.at[(a, *at)], in_sem.at[p, a])

    def send(p):
        at = pl.ds(p * heads, heads)
        return pltpu.make_async_copy(made.at[at], o_ref.at[at], out_sem.at[p])

    for p in range(PIECES):
        for a in range(4):
            fetch(p, a).start()
    place = lax.broadcasted_iota(jnp.int32, (rows, HEAD_DIM), 0) + first_ref[0]
    factor = lax.rsqrt(HEAD_DIM * (place.astype(F32) + 1.0))
    for p in range(PIECES):
        for a in range(4):
            fetch(p, a).wait()
        for h in range(p * heads, (p + 1) * heads):
            at = slice(h * HEAD_DIM, (h + 1) * HEAD_DIM)
            made[h, 0] = held[0, :, at]
            made[h, 1] = held[1, :, at]
            made[h, 2] = (held[2, :, at].astype(F32) * factor).astype(BF16)
            made[h, 3] = held[3, :, at]
        send(p).start()
    for p in range(PIECES):
        send(p).wait()


def pack(first, *arrays):
    rows, width = arrays[0].shape
    shape = (width // HEAD_DIM, 4, rows, HEAD_DIM)
    arrays = [pltpu.with_memory_space_constraint(y, pltpu.HBM) for y in arrays]
    return pl.pallas_call(
        pack_kernel,
        in_specs=[pl.BlockSpec(memory_space=pltpu.SMEM)]
        + [pl.BlockSpec(memory_space=pltpu.HBM)] * 4,
        out_specs=pl.BlockSpec(memory_space=pltpu.HBM),
        out_shape=pltpu.HBM(shape, BF16),
        scratch_shapes=[
            pltpu.VMEM((4, rows, width), BF16),
            pltpu.VMEM(shape, BF16),
            pltpu.SemaphoreType.DMA((PIECES, 4)),
            pltpu.SemaphoreType.DMA((PIECES,)),
        ],
        compiler_params=params(),
        name="pack",
    )(first, *arrays)


def unpack_kernel(x_ref, *refs):
    outs, (made, sem) = refs[:3], refs[3:]
    width = made.shape[2]
    columns = width // PIECES
    heads = columns // HEAD_DIM

    def send(p, a):
        at = (slice(None), pl.ds(p * columns, columns))
        return pltpu.make_async_copy(made.at[(a, *at)], outs[a].at[at], sem.at[p, a])

    for p in range(PIECES):
        for a in range(3):
            for h in range(p * heads, (p + 1) * heads):
                made[a, :, h * HEAD_DIM : (h + 1) * HEAD_DIM] = x_ref[h, a]
            send(p, a).start()
    for p in range(PIECES):
        for a in range(3):
            send(p, a).wait()


def unpack(x):
    heads, n, rows, _ = x.shape
    width = heads * HEAD_DIM
    return pl.pallas_call(
        unpack_kernel,
        in_specs=[pl.BlockSpec(memory_space=pltpu.VMEM)],
        out_specs=[pl.BlockSpec(memory_space=pltpu.HBM)] * n,
        out_shape=[pltpu.HBM((rows, width), x.dtype)] * n,
        scratch_shapes=[
            pltpu.VMEM((n, rows, width), x.dtype),
            pltpu.SemaphoreType.DMA((PIECES, n)),
        ],
        compiler_params=params(),
        name="unpack",
    )(x)


def rows_of(x_ref, a, c=None):
    x = x_ref[:, a] if c is None else x_ref[c * STEP : (c + 1) * STEP, a]
    return x.reshape(-1, HEAD_DIM)


def sums_kernel(me_ref, x_ref, slots_ref):
    kv = dot(rows_of(x_ref, 0), rows_of(x_ref, 1), 0, 0).astype(BF16)
    qg = dot(rows_of(x_ref, 3), rows_of(x_ref, 2), 0, 0).astype(BF16)
    for j in range(slots_ref.shape[0]):
        slots_ref[j] = jnp.where(j > me_ref[0], kv, qg)


def sums(me, x, blocks):
    return pl.pallas_call(
        sums_kernel,
        in_specs=[
            pl.BlockSpec(memory_space=pltpu.SMEM),
            pl.BlockSpec(memory_space=pltpu.VMEM),
        ],
        out_specs=pl.BlockSpec(memory_space=pltpu.VMEM),
        out_shape=jax.ShapeDtypeStruct((blocks, HEAD_DIM, HEAD_DIM), BF16),
        compiler_params=params(),
        name="sums",
    )(me, x)


def near_kernel(x_ref, dq_ref, dk_ref, dv_ref, kv_ref, suf_ref):
    i = pl.program_id(0)
    chunks = suf_ref.shape[0]

    @pl.when(i == 0)
    def _():
        kv_ref[...] = jnp.zeros_like(kv_ref)
        after = jnp.zeros((HEAD_DIM, HEAD_DIM), F32)
        for c in reversed(range(chunks)):
            suf_ref[c] = after
            if c:
                after = after + dot(rows_of(x_ref, 3, c), rows_of(x_ref, 2, c), 0, 0)

    at = pl.ds(i * STEP, STEP)
    k, v, g, q = (x_ref[at, a].reshape(CHUNK, HEAD_DIM) for a in range(4))
    t = lax.broadcasted_iota(jnp.int32, (CHUNK, CHUNK), 0)
    s = lax.broadcasted_iota(jnp.int32, (CHUNK, CHUNK), 1)
    keep = t >= s
    inner = jnp.where(keep, dot(g, v, 1, 1), 0.0).astype(BF16)
    pairs = jnp.where(keep, dot(q, k, 1, 1), 0.0).astype(BF16)
    pre = split(kv_ref[...])
    suf = split(suf_ref[i])
    dq_ref[...] = dot(inner, k, 1, 0) + (dot(g, pre[0], 1, 1) + dot(g, pre[1], 1, 1))
    dk_ref[...] = dot(inner, q, 0, 0) + (dot(v, suf[0], 1, 1) + dot(v, suf[1], 1, 1))
    dv_ref[...] = dot(pairs, g, 0, 0) + (dot(k, suf[0], 1, 0) + dot(k, suf[1], 1, 0))
    kv_ref[...] += dot(k, v, 0, 0)


def near(x):
    chunks = x.shape[0] // STEP
    rows = pl.BlockSpec((CHUNK, HEAD_DIM), lambda i: (i, 0))
    return pl.pallas_call(
        near_kernel,
        grid=(chunks,),
        in_specs=[pl.BlockSpec(memory_space=pltpu.VMEM)],
        out_specs=[rows] * 3,
        out_shape=[jax.ShapeDtypeStruct((chunks * CHUNK, HEAD_DIM), F32)]
        + [pltpu.HBM((chunks * CHUNK, HEAD_DIM), F32)] * 2,
        scratch_shapes=[
            pltpu.VMEM((HEAD_DIM, HEAD_DIM), F32),
            pltpu.VMEM((chunks, HEAD_DIM, HEAD_DIM), F32),
        ],
        compiler_params=params("i"),
        cost_estimate=pl.CostEstimate(flops=3_000_000_000, transcendentals=0, bytes_accessed=8 << 20),
        name="near",
    )(x)


def far_kernel(me_ref, x_ref, got_ref, dq_ref, *refs):
    ins, (o_ref, held, dq_state, dk_state, dv_state, sem) = refs[:2], refs[2:]

    def fetch(a):
        return pltpu.make_async_copy(ins[a], held.at[a], sem.at[a])

    for a in range(2):
        fetch(a).start()
    me = me_ref[0]
    before = jnp.zeros((HEAD_DIM, HEAD_DIM), F32)
    after = jnp.zeros((HEAD_DIM, HEAD_DIM), F32)
    for j in range(got_ref.shape[0]):
        here = got_ref[j].astype(F32)
        before = before + jnp.where(j < me, here, 0.0)
        after = after + jnp.where(j > me, here, 0.0)
    for n, (b, s) in enumerate(zip(split(before), split(after))):
        at = slice(n * HEAD_DIM, (n + 1) * HEAD_DIM)
        dq_state[:, at] = b
        dk_state[:, at] = s
        dv_state[at, :] = s

    def add(out, source, near, state, axis):
        y = rows_of(x_ref, source)
        y = jnp.concatenate([y, y], axis=1)
        value = near[...] + dot(y, state[...], 1, axis)
        o_ref[:, out] = value.astype(BF16).reshape(-1, ROWS, HEAD_DIM)

    add(0, 2, dq_ref, dq_state, 1)
    for a in range(2):
        fetch(a).wait()
    add(1, 1, held.at[0], dk_state, 1)
    add(2, 0, held.at[1], dv_state, 0)


def far(me, x, got, dq, *parts):
    heads = x.shape[0]
    vmem = pl.BlockSpec(memory_space=pltpu.VMEM)
    parts = [pltpu.with_memory_space_constraint(y, pltpu.HBM) for y in parts]
    wide = pltpu.VMEM((HEAD_DIM, 2 * HEAD_DIM), BF16)
    return pl.pallas_call(
        far_kernel,
        in_specs=[pl.BlockSpec(memory_space=pltpu.SMEM), vmem, vmem, vmem]
        + [pl.BlockSpec(memory_space=pltpu.HBM)] * 2,
        out_specs=vmem,
        out_shape=jax.ShapeDtypeStruct((heads, 3, ROWS, HEAD_DIM), BF16),
        scratch_shapes=[
            pltpu.VMEM((2, heads * ROWS, HEAD_DIM), F32),
            wide,
            wide,
            pltpu.VMEM((2 * HEAD_DIM, HEAD_DIM), BF16),
            pltpu.SemaphoreType.DMA((2,)),
        ],
        compiler_params=params(),
        name="far",
    )(me, x, got, dq, *parts)


def swap(x, axis):
    return lax.all_to_all(x, axis, split_axis=0, concat_axis=0, tiled=True)


def local(queries, key_vectors, value_vectors, out_grad):
    me = lax.axis_index(BLOCKS).astype(jnp.int32).reshape(1)
    first = (lax.axis_index(AXES) * ROWS).astype(jnp.int32).reshape(1)
    x = swap(pack(first, key_vectors, value_vectors, out_grad, queries), GROUP)
    got = swap(sums(me, x, lax.axis_size(BLOCKS)), BLOCKS)
    return tuple(unpack(swap(far(me, x, got, *near(x)), GROUP)))


def solution(mesh):
    fine = Mesh(mesh.devices.reshape(8, 64), AXES)
    spec = P(AXES, None)
    return jax.shard_map(
        local, mesh=fine, in_specs=(spec,) * 4, out_specs=(spec,) * 3, check_vma=False
    )
```

```python
import jax
import jax.numpy as jnp
from jax import lax
from jax.experimental import pallas as pl
from jax.experimental.pallas import tpu as pltpu
from jax.sharding import Mesh, PartitionSpec as P

HEAD_DIM = 128
ROWS = 32
CHUNK = 256
STEP = CHUNK // ROWS
TILE = 8
PIECES = 4
BLOCKS = "block"
GROUP = "group"
AXES = (BLOCKS, GROUP)
F32 = jnp.float32
BF16 = jnp.bfloat16


def dot(a, b, ca, cb):
    return lax.dot_general(a, b, (((ca,), (cb,)), ((), ())), preferred_element_type=F32)


def params(*names):
    return pltpu.CompilerParams(
        dimension_semantics=("arbitrary",) * len(names), vmem_limit_bytes=16 * 1024 * 1024
    )


def split(x):
    high = x.astype(BF16)
    return high, (x - high.astype(F32)).astype(BF16)


def pack_kernel(first_ref, *refs):
    ins, (o_ref, held, made, in_sem, out_sem) = refs[:4], refs[4:]
    _, rows, width = held.shape
    columns = width // PIECES
    heads = columns // HEAD_DIM

    def fetch(p, a):
        at = (slice(None), pl.ds(p * columns, columns))
        return pltpu.make_async_copy(ins[a].at[at], held.at[(a, *at)], in_sem.at[p, a])

    def send(p):
        at = pl.ds(p * heads, heads)
        return pltpu.make_async_copy(made.at[at], o_ref.at[at], out_sem.at[p])

    for p in range(PIECES):
        for a in range(4):
            fetch(p, a).start()
    place = lax.broadcasted_iota(jnp.int32, (rows, HEAD_DIM), 0) + first_ref[0]
    factor = lax.rsqrt(HEAD_DIM * (place.astype(F32) + 1.0))
    for p in range(PIECES):
        for a in range(4):
            fetch(p, a).wait()
        for h in range(p * heads, (p + 1) * heads):
            at = slice(h * HEAD_DIM, (h + 1) * HEAD_DIM)
            made[h, 0] = held[0, :, at]
            made[h, 1] = held[1, :, at]
            made[h, 2] = (held[2, :, at].astype(F32) * factor).astype(BF16)
            made[h, 3] = held[3, :, at]
        send(p).start()
    for p in range(PIECES):
        send(p).wait()


def pack(first, *arrays):
    rows, width = arrays[0].shape
    shape = (width // HEAD_DIM, 4, rows, HEAD_DIM)
    arrays = [pltpu.with_memory_space_constraint(y, pltpu.HBM) for y in arrays]
    return pl.pallas_call(
        pack_kernel,
        in_specs=[pl.BlockSpec(memory_space=pltpu.SMEM)]
        + [pl.BlockSpec(memory_space=pltpu.HBM)] * 4,
        out_specs=pl.BlockSpec(memory_space=pltpu.HBM),
        out_shape=pltpu.HBM(shape, BF16),
        scratch_shapes=[
            pltpu.VMEM((4, rows, width), BF16),
            pltpu.VMEM(shape, BF16),
            pltpu.SemaphoreType.DMA((PIECES, 4)),
            pltpu.SemaphoreType.DMA((PIECES,)),
        ],
        compiler_params=params(),
        name="pack",
    )(first, *arrays)


def unpack_kernel(x_ref, *refs):
    outs, sem = refs[:3], refs[3]

    def move(a, r):
        here = x_ref.at[:, a, pl.ds(r * TILE, TILE)]
        return pltpu.make_async_copy(here, outs[a].at[r], sem.at[a, r])

    for a in range(3):
        for r in range(ROWS // TILE):
            move(a, r).start()
    for a in range(3):
        for r in range(ROWS // TILE):
            move(a, r).wait()


def untiled(x):
    n, heads, _, _ = x.shape
    return jnp.transpose(x, (0, 2, 1, 3)).reshape(n * TILE, heads * HEAD_DIM)


def unpack(x):
    heads, n, rows, _ = x.shape
    outs = pl.pallas_call(
        unpack_kernel,
        in_specs=[pl.BlockSpec(memory_space=pltpu.VMEM)],
        out_specs=[pl.BlockSpec(memory_space=pltpu.HBM)] * n,
        out_shape=[pltpu.HBM((rows // TILE, heads, TILE, HEAD_DIM), x.dtype)] * n,
        scratch_shapes=[pltpu.SemaphoreType.DMA((n, rows // TILE))],
        compiler_params=params(),
        name="unpack",
    )(x)
    return [untiled(y) for y in outs]


def rows_of(x_ref, a, c=None):
    x = x_ref[:, a] if c is None else x_ref[c * STEP : (c + 1) * STEP, a]
    return x.reshape(-1, HEAD_DIM)


def sums_kernel(me_ref, x_ref, slots_ref):
    kv = dot(rows_of(x_ref, 0), rows_of(x_ref, 1), 0, 0).astype(BF16)
    qg = dot(rows_of(x_ref, 3), rows_of(x_ref, 2), 0, 0).astype(BF16)
    for j in range(slots_ref.shape[0]):
        slots_ref[j] = jnp.where(j > me_ref[0], kv, qg)


def sums(me, x, blocks):
    return pl.pallas_call(
        sums_kernel,
        in_specs=[
            pl.BlockSpec(memory_space=pltpu.SMEM),
            pl.BlockSpec(memory_space=pltpu.VMEM),
        ],
        out_specs=pl.BlockSpec(memory_space=pltpu.VMEM),
        out_shape=jax.ShapeDtypeStruct((blocks, HEAD_DIM, HEAD_DIM), BF16),
        compiler_params=params(),
        name="sums",
    )(me, x)


def near_kernel(x_ref, dq_ref, dk_ref, dv_ref, kv_ref, suf_ref):
    i = pl.program_id(0)
    chunks = suf_ref.shape[0]

    @pl.when(i == 0)
    def _():
        kv_ref[...] = jnp.zeros_like(kv_ref)
        after = jnp.zeros((HEAD_DIM, HEAD_DIM), F32)
        for c in reversed(range(chunks)):
            suf_ref[c] = after
            if c:
                after = after + dot(rows_of(x_ref, 3, c), rows_of(x_ref, 2, c), 0, 0)

    at = pl.ds(i * STEP, STEP)
    k, v, g, q = (x_ref[at, a].reshape(CHUNK, HEAD_DIM) for a in range(4))
    t = lax.broadcasted_iota(jnp.int32, (CHUNK, CHUNK), 0)
    s = lax.broadcasted_iota(jnp.int32, (CHUNK, CHUNK), 1)
    keep = t >= s
    inner = jnp.where(keep, dot(g, v, 1, 1), 0.0).astype(BF16)
    pairs = jnp.where(keep, dot(q, k, 1, 1), 0.0).astype(BF16)
    pre = split(kv_ref[...])
    suf = split(suf_ref[i])
    dq_ref[...] = dot(inner, k, 1, 0) + (dot(g, pre[0], 1, 1) + dot(g, pre[1], 1, 1))
    dk_ref[...] = dot(inner, q, 0, 0) + (dot(v, suf[0], 1, 1) + dot(v, suf[1], 1, 1))
    dv_ref[...] = dot(pairs, g, 0, 0) + (dot(k, suf[0], 1, 0) + dot(k, suf[1], 1, 0))
    kv_ref[...] += dot(k, v, 0, 0)


def near(x):
    chunks = x.shape[0] // STEP
    rows = pl.BlockSpec((CHUNK, HEAD_DIM), lambda i: (i, 0))
    return pl.pallas_call(
        near_kernel,
        grid=(chunks,),
        in_specs=[pl.BlockSpec(memory_space=pltpu.VMEM)],
        out_specs=[rows] * 3,
        out_shape=[jax.ShapeDtypeStruct((chunks * CHUNK, HEAD_DIM), F32)]
        + [pltpu.HBM((chunks * CHUNK, HEAD_DIM), F32)] * 2,
        scratch_shapes=[
            pltpu.VMEM((HEAD_DIM, HEAD_DIM), F32),
            pltpu.VMEM((chunks, HEAD_DIM, HEAD_DIM), F32),
        ],
        compiler_params=params("i"),
        cost_estimate=pl.CostEstimate(flops=3_000_000_000, transcendentals=0, bytes_accessed=8 << 20),
        name="near",
    )(x)


def far_kernel(me_ref, x_ref, got_ref, dq_ref, *refs):
    ins, (o_ref, held, dq_state, dk_state, dv_state, sem) = refs[:2], refs[2:]

    def fetch(a):
        return pltpu.make_async_copy(ins[a], held.at[a], sem.at[a])

    for a in range(2):
        fetch(a).start()
    me = me_ref[0]
    before = jnp.zeros((HEAD_DIM, HEAD_DIM), F32)
    after = jnp.zeros((HEAD_DIM, HEAD_DIM), F32)
    for j in range(got_ref.shape[0]):
        here = got_ref[j].astype(F32)
        before = before + jnp.where(j < me, here, 0.0)
        after = after + jnp.where(j > me, here, 0.0)
    for n, (b, s) in enumerate(zip(split(before), split(after))):
        at = slice(n * HEAD_DIM, (n + 1) * HEAD_DIM)
        dq_state[:, at] = b
        dk_state[:, at] = s
        dv_state[at, :] = s

    def add(out, source, near, state, axis):
        y = rows_of(x_ref, source)
        y = jnp.concatenate([y, y], axis=1)
        value = near[...] + dot(y, state[...], 1, axis)
        o_ref[:, out] = value.astype(BF16).reshape(-1, ROWS, HEAD_DIM)

    add(0, 2, dq_ref, dq_state, 1)
    for a in range(2):
        fetch(a).wait()
    add(1, 1, held.at[0], dk_state, 1)
    add(2, 0, held.at[1], dv_state, 0)


def far(me, x, got, dq, *parts):
    heads = x.shape[0]
    vmem = pl.BlockSpec(memory_space=pltpu.VMEM)
    parts = [pltpu.with_memory_space_constraint(y, pltpu.HBM) for y in parts]
    wide = pltpu.VMEM((HEAD_DIM, 2 * HEAD_DIM), BF16)
    return pl.pallas_call(
        far_kernel,
        in_specs=[pl.BlockSpec(memory_space=pltpu.SMEM), vmem, vmem, vmem]
        + [pl.BlockSpec(memory_space=pltpu.HBM)] * 2,
        out_specs=vmem,
        out_shape=jax.ShapeDtypeStruct((heads, 3, ROWS, HEAD_DIM), BF16),
        scratch_shapes=[
            pltpu.VMEM((2, heads * ROWS, HEAD_DIM), F32),
            wide,
            wide,
            pltpu.VMEM((2 * HEAD_DIM, HEAD_DIM), BF16),
            pltpu.SemaphoreType.DMA((2,)),
        ],
        compiler_params=params(),
        name="far",
    )(me, x, got, dq, *parts)


def swap(x, axis):
    return lax.all_to_all(x, axis, split_axis=0, concat_axis=0, tiled=True)


def local(queries, key_vectors, value_vectors, out_grad):
    me = lax.axis_index(BLOCKS).astype(jnp.int32).reshape(1)
    first = (lax.axis_index(AXES) * ROWS).astype(jnp.int32).reshape(1)
    x = swap(pack(first, key_vectors, value_vectors, out_grad, queries), GROUP)
    got = swap(sums(me, x, lax.axis_size(BLOCKS)), BLOCKS)
    return tuple(unpack(swap(far(me, x, got, *near(x)), GROUP)))


def solution(mesh):
    fine = Mesh(mesh.devices.reshape(8, 64), AXES)
    spec = P(AXES, None)
    return jax.shard_map(
        local, mesh=fine, in_specs=(spec,) * 4, out_specs=(spec,) * 3, check_vma=False
    )
```
